32 devices in a mesh: rows: 16 (over z, y, x), cols: 2 (over core).
Axes of the slice: x: 2, y: 2, z: 4, core: 2. Of those that a mesh axis runs over, the one named last changes fastest.
Arguments:
- rhs: float32 [8192, 4096], P('rows', 'cols'), may hold values from -6 to 6
- leaf_v: float32 [8192, 256], P(('rows', 'cols')), may hold values from -8 to 8, as said below
- leaf_t: float32 [4096, 256], P('rows'), may hold values from -4 to 4, as said below
- merge_v: float32 [4, 4096, 256], P(None, 'rows'), may hold values from -4 to 4, as said below
- merge_t: float32 [4, 4096, 256], P(None, 'rows'), may hold values from -4 to 4, as said below
Outputs:
- applied: float32 [8192, 4096], P('rows', 'cols')
The draws below stay inside these ranges and needn't reach their ends.
Inputs may be any that keep to these rules, and one draw needn't show every extreme that they name: leaf_v block d is zero above its diagonal and one on it. leaf_t blocks are upper triangular. At level j, merge_v block d is the identity where bit log2(16) - 1 - j of d is 0, and upper triangular where it is 1. merge_t blocks are upper triangular, and at level j the blocks of devices d and d xor 2**(log2(16) - 1 - j) are equal.
All inputs are finite; a program needn't handle non-finite values.
Results may differ from the reference program's by a relative error of at most 0.0001.
Values sent between devices are 32-bit elements; how exact they have to be, the bound alone decides.
A program may use at most 64 MiB of HBM per device.

```python
import jax
import jax.numpy as jnp
from jax import lax

NB = 256
M_DEV = 512
LEVELS = 4
ROWS = 8192
K = 4096
N_ROWS = 16


def draw_leaf_v(key, part):
    shape = (M_DEV * N_ROWS, NB)
    base = jax.random.normal(key, shape, jnp.float32)
    row_pos = jnp.arange(M_DEV * N_ROWS, dtype=jnp.int32)[:, None] % M_DEV
    col_pos = jnp.arange(NB, dtype=jnp.int32)[None, :]
    below = jnp.where(row_pos > col_pos, base / jnp.sqrt(jnp.float32(M_DEV)), 0.0)
    return jnp.where(row_pos == col_pos, 1.0, below).astype(jnp.float32)


def upper_blocks(key, count, diag_lo, diag_hi, spread):
    shape = (count, NB, NB)
    base = jax.random.normal(jax.random.fold_in(key, 1), shape, jnp.float32)
    diagonal = jax.random.uniform(jax.random.fold_in(key, 2), shape, jnp.float32, diag_lo, diag_hi)
    row_pos = jnp.arange(NB, dtype=jnp.int32)[:, None]
    col_pos = jnp.arange(NB, dtype=jnp.int32)[None, :]
    above = jnp.where(row_pos < col_pos, base * (spread / jnp.sqrt(jnp.float32(NB))), 0.0)
    return jnp.where(row_pos == col_pos, diagonal, above)


def draw_leaf_t(key, part):
    return upper_blocks(key, N_ROWS, 0.5, 1.0, 0.5).reshape(N_ROWS * NB, NB)


def draw_merge_v(key, part):
    base = upper_blocks(key, LEVELS * N_ROWS, 0.6, 1.0, 0.7).reshape(LEVELS, N_ROWS, NB, NB)
    device_ids = jnp.arange(N_ROWS, dtype=jnp.int32)
    tree_depth = N_ROWS.bit_length() - 1
    identity = jnp.eye(NB, dtype=jnp.float32)
    layers = []
    for level_index in range(LEVELS):
        stride = 2 ** (tree_depth - 1 - level_index)
        upper_side = (device_ids // stride % 2 == 1)[:, None, None]
        layers.append(jnp.where(upper_side, base[level_index], identity[None, :, :]))
    return jnp.stack(layers).reshape(LEVELS, N_ROWS * NB, NB).astype(jnp.float32)


def draw_merge_t(key, part):
    base = upper_blocks(key, LEVELS * N_ROWS, 0.3, 0.6, 0.5).reshape(LEVELS, N_ROWS, NB, NB)
    device_ids = jnp.arange(N_ROWS, dtype=jnp.int32)
    tree_depth = N_ROWS.bit_length() - 1
    layers = []
    for level_index in range(LEVELS):
        stride = 2 ** (tree_depth - 1 - level_index)
        owner = device_ids // (2 * stride) * (2 * stride) + device_ids % stride
        layers.append(jnp.take(base[level_index], owner, axis=0))
    return jnp.stack(layers).reshape(LEVELS, N_ROWS * NB, NB)


def shard_levels(rng, shape, shards, least, high):
    level = 1.0
    for position, blocks in shards:
        steps = jax.random.uniform(jax.random.fold_in(jax.random.fold_in(rng, 6), position), (blocks,), jnp.float32, least / len(shards), high / len(shards))
        level = level * jnp.repeat(jnp.exp(steps), shape[position] // blocks).reshape((-1,) + (1,) * (len(shape) - 1 - position))
    return level


def noise(own_key, shape, deviation, most, pieces=(), kind=jnp.bfloat16):
    level = shard_levels(own_key, shape, pieces, -0.22, 0.18) if pieces else 1.0
    entries = jax.random.normal(own_key, shape, jnp.float32) * deviation * level
    return jnp.minimum(jnp.maximum(entries, -most), most).astype(kind)


def setup_inputs(seed: int = 0) -> dict:
    key_of = jax.random.split(jax.random.key(seed), 6)
    rhs = noise(key_of[0], (ROWS, K), 1.0, 6.0, ((0, 16), (1, 2)), jnp.float32)
    leaf_v = draw_leaf_v(jax.random.fold_in(key_of[5], 71), 0)
    leaf_t = draw_leaf_t(jax.random.fold_in(key_of[5], 71), 0)
    merge_v = draw_merge_v(jax.random.fold_in(key_of[5], 71), 0)
    merge_t = draw_merge_t(jax.random.fold_in(key_of[5], 71), 0)
    return {"rhs": rhs, "leaf_v": leaf_v, "leaf_t": leaf_t, "merge_v": merge_v, "merge_t": merge_t}


HIGH = lax.Precision.HIGHEST


def reference(rhs, leaf_v, leaf_t, merge_v, merge_t):
    blocks = rhs.reshape(N_ROWS, M_DEV, K)
    upper_rows = blocks[:, :NB]
    lower_rows = blocks[:, NB:]
    device_ids = jnp.arange(N_ROWS, dtype=jnp.int32)
    tree_depth = N_ROWS.bit_length() - 1
    for level_index in range(LEVELS):
        distance_bit = tree_depth - 1 - level_index
        partner_ids = jnp.bitwise_xor(device_ids, jnp.int32(2 ** distance_bit))
        merge_block = merge_v[level_index].reshape(N_ROWS, NB, NB)
        merge_tri = merge_t[level_index].reshape(N_ROWS, NB, NB)
        own_terms = jnp.einsum("dnk,dnj->dkj", merge_block, upper_rows, precision=HIGH)
        summed = own_terms + own_terms[partner_ids]
        weights = jnp.einsum("dkm,dmj->dkj", merge_tri, summed, precision=HIGH)
        upper_rows = upper_rows - jnp.einsum("dnk,dkj->dnj", merge_block, weights, precision=HIGH)
    stacked = jnp.concatenate([upper_rows, lower_rows], axis=1)
    leaf_blocks = leaf_v.reshape(N_ROWS, M_DEV, NB)
    leaf_tris = leaf_t.reshape(N_ROWS, NB, NB)

    def leaf_apply(items):
        block, refl, tri = items
        proj = jnp.dot(refl.T, block, precision=HIGH)
        inner = jnp.dot(tri, proj, precision=HIGH)
        return block - jnp.dot(refl, inner, precision=HIGH)

    result = lax.map(leaf_apply, (stacked, leaf_blocks, leaf_tris))
    return result.reshape(ROWS, K)
```

```python
import functools

import jax
import jax.numpy as jnp
from jax import lax
from jax.experimental import pallas as pl
from jax.experimental.pallas import tpu as pltpu
from jax.sharding import PartitionSpec as P

MESH = pl.DeviceIdType.MESH
WIDTH = 128
LOOK = 3
FIRST_LAG = 2


def split_rows(w):
    hi = w.astype(jnp.bfloat16)
    lo = (w - hi.astype(jnp.float32)).astype(jnp.bfloat16)
    return jnp.concatenate([hi, lo], axis=0)


def split_cols(x):
    hi = x.astype(jnp.bfloat16)
    lo = (x - hi.astype(jnp.float32)).astype(jnp.bfloat16)
    return jnp.concatenate([hi, lo], axis=1)


def times(w_ref, x):
    m, n = w_ref.shape[0] // 2, x.shape[1]
    p = jnp.dot(w_ref[...], split_cols(x), preferred_element_type=jnp.float32)
    return (p[:m, :n] + p[:m, n:]) + (p[m:, :n] + p[m:, n:])


def kernel(
    rhs, leaf_v, leaf_t, merge_v, merge_t, out,
    x, sent, got, mv, mt, lv, lt, v2, vt2, t2, l2, lt2, r2,
    up_sem, low_sem, out_sem, mv_sem, mt_sem, lv_sem, lt_sem, leaf_send, leaf_recv, send_sem, recv_sem,
):
    levels, width = merge_v.shape[0], leaf_t.shape[1]
    chunks = x.shape[0]
    depth = lax.axis_size("rows").bit_length() - 1
    row, col = lax.axis_index("rows"), lax.axis_index("cols")
    partners = []
    for j in range(levels):
        stride = 1 << (depth - 1 - j)
        partners.append(row + stride * (1 - 2 * ((row // stride) % 2)))

    def columns(c):
        return pl.ds(pl.multiple_of(c * WIDTH, WIDTH), WIDTH)

    def upper_copy(c):
        return pltpu.make_async_copy(rhs.at[pl.ds(0, width), columns(c)], x.at[c, pl.ds(0, width)], up_sem.at[c])

    def lower_copy(c):
        low = pl.ds(width, x.shape[1] - width)
        return pltpu.make_async_copy(rhs.at[low, columns(c)], x.at[c, low], low_sem.at[c])

    def out_copy(c):
        return pltpu.make_async_copy(x.at[c], out.at[:, columns(c)], out_sem.at[c])

    def exchange(j, c):
        return pltpu.make_async_remote_copy(
            src_ref=sent.at[j, c], dst_ref=got.at[j, c],
            send_sem=send_sem.at[j, c], recv_sem=recv_sem.at[j, c],
            device_id=(partners[j], col), device_id_type=MESH,
        )

    half = leaf_v.shape[0]
    own_half = pl.ds(pl.multiple_of(col * half, half), half)
    leaf_here = pltpu.make_async_copy(leaf_v, lv.at[own_half], lv_sem)
    leaf_there = pltpu.make_async_remote_copy(
        src_ref=leaf_v, dst_ref=lv.at[own_half], send_sem=leaf_send, recv_sem=leaf_recv,
        device_id=(row, 1 - col), device_id_type=MESH,
    )
    mv_copies = [pltpu.make_async_copy(merge_v.at[j], mv.at[j], mv_sem.at[j]) for j in range(levels)]
    mt_copies = [pltpu.make_async_copy(merge_t.at[j], mt.at[j], mt_sem.at[j]) for j in range(levels)]
    lt_copy = pltpu.make_async_copy(leaf_t, lt, lt_sem)

    mv_copies[0].start()
    for c in range(LOOK):
        upper_copy(c).start()
    for j in range(levels):
        mt_copies[j].start()
        if j > 0:
            mv_copies[j].start()
    leaf_here.start()
    lt_copy.start()

    def load(c, carry):
        upper_copy(c).start()
        return carry

    def load_low(c, carry):
        lower_copy(c).start()
        return carry

    lax.fori_loop(LOOK, chunks, load, 0)
    lax.fori_loop(0, chunks, load_low, 0)

    barrier = pltpu.get_barrier_semaphore()
    for j in range(levels):
        pl.semaphore_signal(barrier, inc=1, device_id=(partners[j], col), device_id_type=MESH)
    pl.semaphore_signal(barrier, inc=1, device_id=(row, 1 - col), device_id_type=MESH)

    def prepare_v(j):
        mv_copies[j].wait()
        v = mv[j]
        vt2[j] = split_rows(v.T)
        v2[j] = split_rows(v)

    def prepare_t(j):
        mt_copies[j].wait()
        t2[j] = split_rows(mt[j])

    def first(c):
        upper_copy(c).wait()
        sent[0, c] = times(vt2.at[0], x[c, :width])
        exchange(0, c).start()

    prepare_v(0)
    pl.semaphore_wait(barrier, levels + 1)
    for c in range(LOOK):
        first(c)
    leaf_there.start()
    prepare_t(0)
    for j in range(1, levels):
        prepare_v(j)
        prepare_t(j)
    leaf_here.wait()
    lt_copy.wait()
    r2[...] = split_rows(lt[...])
    leaf_there.wait()
    whole = lv[...]
    l2[...] = split_rows(whole)
    lt2[...] = split_rows(whole.T)

    def merged(j, c):
        exchange(j, c).wait_recv()
        weights = times(t2.at[j], sent[j, c] + got[j, c])
        return x[c, :width] - times(v2.at[j], weights)

    def middle(j, c):
        upper = merged(j, c)
        x[c, :width] = upper
        sent[j + 1, c] = times(vt2.at[j + 1], upper)
        exchange(j + 1, c).start()

    def last(c):
        lower_copy(c).wait()
        x[c, :width] = merged(levels - 1, c)
        block = x[c]
        inner = times(r2, times(lt2, block))
        x[c] = block - times(l2, inner)
        out_copy(c).start()

    lags = [0] + [FIRST_LAG + j for j in range(levels - 1)]

    def step(t, carry):
        @pl.when(t + LOOK < chunks)
        def _():
            first(t + LOOK)

        for j in reversed(range(levels)):
            c = t - lags[j]

            @pl.when((c >= 0) & (c < chunks))
            def _():
                if j == levels - 1:
                    last(c)
                else:
                    middle(j, c)

        return carry

    lax.fori_loop(0, chunks + lags[-1], step, 0)

    def drain(c, carry):
        for j in range(levels):
            exchange(j, c).wait_send()
        out_copy(c).wait()
        return carry

    lax.fori_loop(0, chunks, drain, 0)


def body(rhs, leaf_v, leaf_t, merge_v, merge_t):
    rows, cols = rhs.shape
    levels, width = merge_v.shape[0], leaf_t.shape[1]
    chunks = cols // WIDTH
    f32, bf16 = jnp.float32, jnp.bfloat16
    dma = pltpu.SemaphoreType.DMA
    anywhere = pl.BlockSpec(memory_space=pl.ANY)
    return pl.pallas_call(
        kernel,
        out_shape=jax.ShapeDtypeStruct((rows, cols), f32),
        in_specs=[anywhere] * 5,
        out_specs=anywhere,
        scratch_shapes=[
            pltpu.VMEM((chunks, rows, WIDTH), f32),
            pltpu.VMEM((levels, chunks, width, WIDTH), f32),
            pltpu.VMEM((levels, chunks, width, WIDTH), f32),
            pltpu.VMEM((levels, width, width), f32),
            pltpu.VMEM((levels, width, width), f32),
            pltpu.VMEM((rows, width), f32),
            pltpu.VMEM((width, width), f32),
            pltpu.VMEM((levels, 2 * width, width), bf16),
            pltpu.VMEM((levels, 2 * width, width), bf16),
            pltpu.VMEM((levels, 2 * width, width), bf16),
            pltpu.VMEM((2 * rows, width), bf16),
            pltpu.VMEM((2 * width, rows), bf16),
            pltpu.VMEM((2 * width, width), bf16),
            dma((chunks,)),
            dma((chunks,)),
            dma((chunks,)),
            dma((levels,)),
            dma((levels,)),
            dma,
            dma,
            dma,
            dma,
            dma((levels, chunks)),
            dma((levels, chunks)),
        ],
        compiler_params=pltpu.CompilerParams(
            collective_id=0, has_side_effects=True, vmem_limit_bytes=48 * 1024 * 1024
        ),
    )(rhs, leaf_v, leaf_t, merge_v, merge_t)


def solution(mesh):
    return jax.shard_map(
        body,
        mesh=mesh,
        in_specs=(
            P("rows", "cols"),
            P(("rows", "cols"), None),
            P("rows", None),
            P(None, "rows", None),
            P(None, "rows", None),
        ),
        out_specs=P("rows", "cols"),
        check_vma=False,
    )
```

```python
import functools

import jax
import jax.numpy as jnp
from jax import lax
from jax.experimental import pallas as pl
from jax.experimental.pallas import tpu as pltpu
from jax.sharding import PartitionSpec as P

MESH = pl.DeviceIdType.MESH
WIDTH = 256
OWN_LOOK = 4
FAR_LOOK = 2
LAG = 2


def halves(x):
    hi = x.astype(jnp.bfloat16)
    return hi, (x - hi.astype(jnp.float32)).astype(jnp.bfloat16)


def split(w):
    hi, lo = halves(w)
    return jnp.concatenate([hi, hi, lo], axis=1)


def times(w_ref, x):
    hi, lo = halves(x)
    return jnp.dot(w_ref[...], jnp.concatenate([hi, lo, hi], axis=0), preferred_element_type=jnp.float32)


def kernel(
    rhs, leaf_v, leaf_t, merge_v, merge_t, out,
    x, sent, got, mv, mt, lv, lt, far, v2, vt2, t2, far_v2, far_vt2, far_t2, l2, lt2, r2,
    up_sem, low_sem, out_sem, mv_sem, mt_sem, lv_sem, lt_sem, leaf_send, leaf_recv, far_send, far_recv, send_sem, recv_sem,
):
    levels, width = merge_v.shape[0], leaf_t.shape[1]
    chunks = x.shape[0]
    depth = lax.axis_size("rows").bit_length() - 1
    row, col = lax.axis_index("rows"), lax.axis_index("cols")
    partners, bits = [], []
    for j in range(levels):
        stride = 1 << (depth - 1 - j)
        bits.append((row // stride) % 2)
        partners.append(row + stride * (1 - 2 * bits[j]))
    beside = partners[1]
    across = partners[0] + partners[1] - row
    inner = bits[0] != bits[1]
    outer = bits[0] == bits[1]

    def columns(c):
        return pl.ds(pl.multiple_of(c * WIDTH, WIDTH), WIDTH)

    def upper_copy(c):
        return pltpu.make_async_copy(rhs.at[pl.ds(0, width), columns(c)], x.at[c, pl.ds(0, width)], up_sem.at[c])

    def lower_copy(c):
        low = pl.ds(width, x.shape[1] - width)
        return pltpu.make_async_copy(rhs.at[low, columns(c)], x.at[c, low], low_sem.at[c])

    def out_copy(c):
        return pltpu.make_async_copy(x.at[c], out.at[:, columns(c)], out_sem.at[c])

    def remote(src, slot, c, device):
        return pltpu.make_async_remote_copy(
            src_ref=src, dst_ref=got.at[slot, c],
            send_sem=send_sem.at[slot, c], recv_sem=recv_sem.at[slot, c],
            device_id=(device, col), device_id_type=MESH,
        )

    def cross(slot, c):
        return remote(sent.at[slot, c], slot, c, across)

    def hand_over(c):
        return remote(x.at[c, pl.ds(0, width)], 2, c, beside)

    def hand_back(c):
        return remote(sent.at[2, c], 2, c, beside)

    def exchange(j, c):
        return remote(sent.at[j + 1, c], j + 1, c, partners[j])

    half = leaf_v.shape[0]
    own_half = pl.ds(pl.multiple_of(col * half, half), half)
    leaf_here = pltpu.make_async_copy(leaf_v, lv.at[own_half], lv_sem)
    leaf_there = pltpu.make_async_remote_copy(
        src_ref=leaf_v, dst_ref=lv.at[own_half], send_sem=leaf_send, recv_sem=leaf_recv,
        device_id=(row, 1 - col), device_id_type=MESH,
    )
    mv_copies = [pltpu.make_async_copy(merge_v.at[j], mv.at[j], mv_sem.at[j]) for j in range(levels)]
    mt_copies = [pltpu.make_async_copy(merge_t.at[j], mt.at[j], mt_sem.at[j]) for j in range(levels)]
    lt_copy = pltpu.make_async_copy(leaf_t, lt, lt_sem)
    far_copies = [
        pltpu.make_async_remote_copy(
            src_ref=src, dst_ref=far.at[i], send_sem=far_send.at[i], recv_sem=far_recv.at[i],
            device_id=(beside, col), device_id_type=MESH,
        )
        for i, src in enumerate((merge_v.at[0], merge_t.at[0], merge_v.at[1]))
    ]

    mv_copies[0].start()
    barrier = pltpu.get_barrier_semaphore()
    for device in [across, beside] + partners[2:]:
        pl.semaphore_signal(barrier, inc=1, device_id=(device, col), device_id_type=MESH)
    pl.semaphore_signal(barrier, inc=1, device_id=(row, 1 - col), device_id_type=MESH)

    def load(c, carry):
        upper_copy(c).start()
        return carry

    def load_low(c, carry):
        lower_copy(c).start()
        return carry

    lax.fori_loop(0, chunks, load, 0)
    for j in range(levels):
        mt_copies[j].start()
        if j > 0:
            mv_copies[j].start()
    leaf_here.start()
    lt_copy.start()
    lax.fori_loop(0, chunks, load_low, 0)

    def prepare_v(j):
        mv_copies[j].wait()
        v = mv[j]
        vt2[j] = split(v.T)
        v2[j] = split(v)

    def prepare_t(j):
        mt_copies[j].wait()
        t2[j] = split(mt[j])

    def prepare_far(i):
        far_copies[i].wait_recv()
        if i == 1:
            far_t2[...] = split(far[1])
        else:
            v = far[i]
            far_vt2[i // 2] = split(v.T)
            far_v2[i // 2] = split(v)

    def first_own(c):
        upper_copy(c).wait()
        sent[0, c] = times(vt2.at[0], x[c, :width])
        cross(0, c).start()

    def first_far(c):
        hand_back(c).wait_recv()
        sent[1, c] = times(far_vt2.at[0], got[2, c])
        cross(1, c).start()

    prepare_v(0)
    pl.semaphore_wait(barrier, levels + 1)

    def give(c, carry):
        upper_copy(c).wait()
        hand_over(c).start()
        return carry

    @pl.when(outer)
    def _():
        far_copies[0].start()
        give(0, 0)
        give(1, 0)
        far_copies[1].start()
        far_copies[2].start()
        lax.fori_loop(2, chunks, give, 0)

    @pl.when(inner)
    def _():
        for c in range(OWN_LOOK):
            first_own(c)

    leaf_there.start()
    prepare_t(0)
    for j in range(1, levels):
        prepare_v(j)
        prepare_t(j)
    leaf_here.wait()
    lt_copy.wait()
    r2[...] = split(lt[...])

    @pl.when(inner)
    def _():
        prepare_far(0)
        for c in range(FAR_LOOK):
            first_far(c)
        prepare_far(1)
        prepare_far(2)

    leaf_there.wait()
    whole = lv[...]
    l2[...] = split(whole)
    lt2[...] = split(whole.T)

    def send_on(j, c, upper):
        x[c, :width] = upper
        sent[j + 1, c] = times(vt2.at[j], upper)
        exchange(j, c).start()

    def two_levels(c):
        cross(0, c).wait_recv()
        cross(1, c).wait_recv()
        far_w = times(far_t2, sent[1, c] + got[0, c])
        own_w = times(t2.at[0], sent[0, c] + got[1, c])
        far_u = got[2, c] - times(far_v2.at[0], far_w)
        own_u = x[c, :width] - times(v2.at[0], own_w)
        both = times(vt2.at[1], own_u) + times(far_vt2.at[1], far_u)
        pair_w = times(t2.at[1], both)
        sent[2, c] = far_u - times(far_v2.at[1], pair_w)
        hand_back(c).start()
        send_on(2, c, own_u - times(v2.at[1], pair_w))

    def take_back(c):
        hand_over(c).wait()
        send_on(2, c, got[2, c])

    def merged(j, c):
        exchange(j, c).wait_recv()
        weights = times(t2.at[j], sent[j + 1, c] + got[j + 1, c])
        return x[c, :width] - times(v2.at[j], weights)

    def last(c):
        lower_copy(c).wait()
        x[c, :width] = merged(levels - 1, c)
        block = x[c]
        inner_w = times(r2, times(lt2, block))
        x[c] = block - times(l2, inner_w)
        out_copy(c).start()

    def step(t, carry):
        @pl.when(inner & (t + OWN_LOOK < chunks))
        def _():
            first_own(t + OWN_LOOK)

        @pl.when(inner & (t + FAR_LOOK < chunks))
        def _():
            first_far(t + FAR_LOOK)

        for j in reversed(range(2, levels)):
            c = t - (j - 1) * LAG

            @pl.when((c >= 0) & (c < chunks))
            def _():
                if j == levels - 1:
                    last(c)
                else:
                    send_on(j + 1, c, merged(j, c))

        @pl.when(inner & (t < chunks))
        def _():
            two_levels(t)

        @pl.when(outer & (t < chunks))
        def _():
            take_back(t)

        return carry

    lax.fori_loop(0, chunks + (levels - 2) * LAG, step, 0)

    def drain(c, carry):
        for j in range(2, levels):
            exchange(j, c).wait_send()
        out_copy(c).wait()
        return carry

    def drain_inner(c, carry):
        cross(0, c).wait_send()
        cross(1, c).wait_send()
        hand_back(c).wait_send()
        return carry

    @pl.when(inner)
    def _():
        lax.fori_loop(0, chunks, drain_inner, 0)

    @pl.when(outer)
    def _():
        for copy in far_copies:
            copy.wait_send()

    lax.fori_loop(0, chunks, drain, 0)


def body(rhs, leaf_v, leaf_t, merge_v, merge_t):
    rows, cols = rhs.shape
    levels, width = merge_v.shape[0], leaf_t.shape[1]
    chunks = cols // WIDTH
    f32, bf16 = jnp.float32, jnp.bfloat16
    dma = pltpu.SemaphoreType.DMA
    anywhere = pl.BlockSpec(memory_space=pltpu.HBM)
    return pl.pallas_call(
        kernel,
        out_shape=jax.ShapeDtypeStruct((rows, cols), f32),
        in_specs=[anywhere] * 5,
        out_specs=anywhere,
        scratch_shapes=[
            pltpu.VMEM((chunks, rows, WIDTH), f32),
            pltpu.VMEM((levels + 1, chunks, width, WIDTH), f32),
            pltpu.VMEM((levels + 1, chunks, width, WIDTH), f32),
            pltpu.VMEM((levels, width, width), f32),
            pltpu.VMEM((levels, width, width), f32),
            pltpu.VMEM((rows, width), f32),
            pltpu.VMEM((width, width), f32),
            pltpu.VMEM((3, width, width), f32),
            pltpu.VMEM((levels, width, 3 * width), bf16),
            pltpu.VMEM((levels, width, 3 * width), bf16),
            pltpu.VMEM((levels, width, 3 * width), bf16),
            pltpu.VMEM((2, width, 3 * width), bf16),
            pltpu.VMEM((2, width, 3 * width), bf16),
            pltpu.VMEM((width, 3 * width), bf16),
            pltpu.VMEM((rows, 3 * width), bf16),
            pltpu.VMEM((width, 3 * rows), bf16),
            pltpu.VMEM((width, 3 * width), bf16),
            dma((chunks,)),
            dma((chunks,)),
            dma((chunks,)),
            dma((levels,)),
            dma((levels,)),
            dma,
            dma,
            dma,
            dma,
            dma((3,)),
            dma((3,)),
            dma((levels + 1, chunks)),
            dma((levels + 1, chunks)),
        ],
        compiler_params=pltpu.CompilerParams(
            collective_id=0, has_side_effects=True, vmem_limit_bytes=62 * 1024 * 1024
        ),
    )(rhs, leaf_v, leaf_t, merge_v, merge_t)


def solution(mesh):
    return jax.shard_map(
        body,
        mesh=mesh,
        in_specs=(
            P("rows", "cols"),
            P(("rows", "cols"), None),
            P("rows", None),
            P(None, "rows", None),
            P(None, "rows", None),
        ),
        out_specs=P("rows", "cols"),
        check_vma=False,
    )
```

```python
import functools

import jax
import jax.numpy as jnp
from jax import lax
from jax.experimental import pallas as pl
from jax.experimental.pallas import tpu as pltpu
from jax.sharding import PartitionSpec as P

MESH = pl.DeviceIdType.MESH
WIDTH = 128
SINGLES = 4
OWN_LOOK = 4
FAR_LOOK = 3
LAG = 2


def halves(x):
    hi = x.astype(jnp.bfloat16)
    return hi, (x - hi.astype(jnp.float32)).astype(jnp.bfloat16)


def split(w):
    hi, lo = halves(w)
    return jnp.concatenate([hi, hi, lo], axis=1)


def times(w_ref, x):
    hi, lo = halves(x)
    return jnp.dot(w_ref[...], jnp.concatenate([hi, lo, hi], axis=0), preferred_element_type=jnp.float32)


def kernel(
    rhs, leaf_v, leaf_t, merge_v, merge_t, out,
    x, sent, got, mv, mt, lv, lt, far, v2, vt2, far_v2, far_vt2, l2, lt2,
    up_sem, low_sem, out_sem, mv_sem, mt_sem, lv_sem, lt_sem, leaf_send, leaf_recv, far_send, far_recv, send_sem, recv_sem,
):
    levels, width = merge_v.shape[0], leaf_t.shape[1]
    chunks = x.shape[0]
    depth = lax.axis_size("rows").bit_length() - 1
    row, col = lax.axis_index("rows"), lax.axis_index("cols")
    partners, bits = [], []
    for j in range(levels):
        stride = 1 << (depth - 1 - j)
        bits.append((row // stride) % 2)
        partners.append(row + stride * (1 - 2 * bits[j]))
    beside = partners[1]
    across = partners[0] + partners[1] - row
    inner = bits[0] != bits[1]
    outer = bits[0] == bits[1]

    def columns(c):
        return pl.ds(pl.multiple_of(c * WIDTH, WIDTH), WIDTH)

    def upper_copy(c):
        return pltpu.make_async_copy(rhs.at[pl.ds(0, width), columns(c)], x.at[c, pl.ds(0, width)], up_sem.at[c])

    def lower_copy(c):
        low = pl.ds(width, x.shape[1] - width)
        return pltpu.make_async_copy(rhs.at[low, columns(c)], x.at[c, low], low_sem.at[c])

    def out_copy(c):
        return pltpu.make_async_copy(x.at[c], out.at[:, columns(c)], out_sem.at[c])

    def remote(src, slot, c, device):
        return pltpu.make_async_remote_copy(
            src_ref=src, dst_ref=got.at[slot, c],
            send_sem=send_sem.at[slot, c], recv_sem=recv_sem.at[slot, c],
            device_id=(device, col), device_id_type=MESH,
        )

    def cross(slot, c):
        return remote(sent.at[slot, c], slot, c, across)

    def hand_over(c):
        return remote(x.at[c, pl.ds(0, width)], 2, c, beside)

    def hand_back(c):
        return remote(sent.at[2, c], 2, c, beside)

    def exchange(j, c):
        return remote(sent.at[j + 1, c], j + 1, c, partners[j])

    half = leaf_v.shape[0]
    own_half = pl.ds(pl.multiple_of(col * half, half), half)
    leaf_here = pltpu.make_async_copy(leaf_v, lv.at[own_half], lv_sem)
    leaf_there = pltpu.make_async_remote_copy(
        src_ref=leaf_v, dst_ref=lv.at[own_half], send_sem=leaf_send, recv_sem=leaf_recv,
        device_id=(row, 1 - col), device_id_type=MESH,
    )
    mv_copies = [pltpu.make_async_copy(merge_v.at[j], mv.at[j], mv_sem.at[j]) for j in range(levels)]
    mt_copies = [pltpu.make_async_copy(merge_t.at[j], mt.at[j], mt_sem.at[j]) for j in range(levels)]
    lt_copy = pltpu.make_async_copy(leaf_t, lt, lt_sem)
    far_copies = [
        pltpu.make_async_remote_copy(
            src_ref=src, dst_ref=far.at[i], send_sem=far_send.at[i], recv_sem=far_recv.at[i],
            device_id=(beside, col), device_id_type=MESH,
        )
        for i, src in enumerate((merge_v.at[0], merge_t.at[0], merge_v.at[1]))
    ]

    mv_copies[0].start()
    barrier = pltpu.get_barrier_semaphore()
    for device in [across, beside] + partners[2:]:
        pl.semaphore_signal(barrier, inc=1, device_id=(device, col), device_id_type=MESH)
    pl.semaphore_signal(barrier, inc=1, device_id=(row, 1 - col), device_id_type=MESH)

    def load(c, carry):
        upper_copy(c).start()
        return carry

    def load_low(c, carry):
        lower_copy(c).start()
        return carry

    lax.fori_loop(0, chunks, load, 0)
    for j in range(levels):
        mt_copies[j].start()
        if j > 0:
            mv_copies[j].start()
    leaf_here.start()
    lt_copy.start()
    lax.fori_loop(0, chunks, load_low, 0)

    def prepare_v(j):
        mv_copies[j].wait()
        v = mv[j]
        vt2[j] = split(v.T)
        v2[j] = split(v)

    def prepare_t(j):
        mt_copies[j].wait()
        v2[j] = split(times(v2.at[j], mt[j]))

    def prepare_far(i):
        far_copies[i].wait_recv()
        if i == 1:
            far_v2[0] = split(times(far_v2.at[0], far[1]))
        else:
            v = far[i]
            far_vt2[i // 2] = split(v.T)
            far_v2[i // 2] = split(v)
            if i == 2:
                far_v2[1] = split(times(far_v2.at[1], mt[1]))

    singles = min(SINGLES, chunks)
    pairs = (chunks - singles) // 2
    units = pairs + chunks - 2 * pairs

    def read(ref, c, n):
        return jnp.concatenate([ref[c + i] for i in range(n)], axis=1)

    def write(ref, c, n, value):
        for i in range(n):
            ref[c + i] = value[:, i * WIDTH : (i + 1) * WIDTH]

    def read_upper(c, n):
        return jnp.concatenate([x[c + i, :width] for i in range(n)], axis=1)

    def write_upper(c, n, value):
        for i in range(n):
            x[c + i, :width] = value[:, i * WIDTH : (i + 1) * WIDTH]

    def on_unit(stage, u, take):
        take = take & (u >= 0) & (u < units)

        @pl.when(take & (u < pairs))
        def _():
            stage(2 * u, 2)

        @pl.when(take & (u >= pairs))
        def _():
            stage(pairs + u, 1)

    def first_own(c, n):
        for i in range(n):
            upper_copy(c + i).wait()
        write(sent.at[0], c, n, times(vt2.at[0], read_upper(c, n)))
        for i in range(n):
            cross(0, c + i).start()

    def first_far(c, n):
        for i in range(n):
            hand_back(c + i).wait_recv()
        write(sent.at[1], c, n, times(far_vt2.at[0], read(got.at[2], c, n)))
        for i in range(n):
            cross(1, c + i).start()

    prepare_v(0)
    pl.semaphore_wait(barrier, levels + 1)

    def give(c, carry):
        upper_copy(c).wait()
        hand_over(c).start()
        return carry

    @pl.when(outer)
    def _():
        far_copies[0].start()
        give(0, 0)
        give(1, 0)
        far_copies[1].start()
        give(2, 0)
        give(3, 0)
        far_copies[2].start()
        lax.fori_loop(4, chunks, give, 0)

    @pl.when(inner)
    def _():
        for u in range(OWN_LOOK):
            first_own(2 * u, 2)

    leaf_there.start()
    prepare_t(0)
    for j in range(1, levels):
        prepare_v(j)
        prepare_t(j)
    leaf_here.wait()
    lt_copy.wait()

    @pl.when(inner)
    def _():
        prepare_far(0)
        for u in range(FAR_LOOK):
            first_far(2 * u, 2)
        prepare_far(1)
        prepare_far(2)

    leaf_there.wait()
    whole = lv[...]
    l2[...] = split(whole)
    l2[...] = split(times(l2, lt[...]))
    lt2[...] = split(whole.T)

    def send_on(j, c, n, upper):
        write_upper(c, n, upper)
        write(sent.at[j + 1], c, n, times(vt2.at[j], upper))
        for i in range(n):
            exchange(j, c + i).start()

    def two_levels(c, n):
        for i in range(n):
            cross(0, c + i).wait_recv()
            cross(1, c + i).wait_recv()
        far_sum = read(sent.at[1], c, n) + read(got.at[0], c, n)
        own_sum = read(sent.at[0], c, n) + read(got.at[1], c, n)
        far_u = read(got.at[2], c, n) - times(far_v2.at[0], far_sum)
        own_u = read_upper(c, n) - times(v2.at[0], own_sum)
        both = times(vt2.at[1], own_u) + times(far_vt2.at[1], far_u)
        write(sent.at[2], c, n, far_u - times(far_v2.at[1], both))
        for i in range(n):
            hand_back(c + i).start()
        send_on(2, c, n, own_u - times(v2.at[1], both))

    def take_back(c, n):
        for i in range(n):
            hand_over(c + i).wait()
        send_on(2, c, n, read(got.at[2], c, n))

    def merged(j, c, n):
        for i in range(n):
            exchange(j, c + i).wait_recv()
        return read_upper(c, n) - times(v2.at[j], read(sent.at[j + 1], c, n) + read(got.at[j + 1], c, n))

    def middle(j, c, n):
        send_on(j + 1, c, n, merged(j, c, n))

    def last(c, n):
        for i in range(n):
            lower_copy(c + i).wait()
        write_upper(c, n, merged(levels - 1, c, n))
        block = read(x, c, n)
        write(x, c, n, block - times(l2, times(lt2, block)))
        for i in range(n):
            out_copy(c + i).start()

    def step(t, carry):
        on_unit(first_own, t + OWN_LOOK, inner)
        on_unit(first_far, t + FAR_LOOK, inner)
        for j in reversed(range(2, levels)):
            stage = last if j == levels - 1 else functools.partial(middle, j)
            on_unit(stage, t - (j - 1) * LAG, True)
        on_unit(two_levels, t, inner)
        on_unit(take_back, t, outer)
        return carry

    lax.fori_loop(0, units + (levels - 2) * LAG, step, 0)

    def drain(c, carry):
        for j in range(2, levels):
            exchange(j, c).wait_send()
        out_copy(c).wait()
        return carry

    def drain_inner(c, carry):
        cross(0, c).wait_send()
        cross(1, c).wait_send()
        hand_back(c).wait_send()
        return carry

    @pl.when(inner)
    def _():
        lax.fori_loop(0, chunks, drain_inner, 0)

    @pl.when(outer)
    def _():
        for copy in far_copies:
            copy.wait_send()

    lax.fori_loop(0, chunks, drain, 0)


def body(rhs, leaf_v, leaf_t, merge_v, merge_t):
    rows, cols = rhs.shape
    levels, width = merge_v.shape[0], leaf_t.shape[1]
    chunks = cols // WIDTH
    f32, bf16 = jnp.float32, jnp.bfloat16
    dma = pltpu.SemaphoreType.DMA
    anywhere = pl.BlockSpec(memory_space=pltpu.HBM)
    return pl.pallas_call(
        kernel,
        out_shape=jax.ShapeDtypeStruct((rows, cols), f32),
        in_specs=[anywhere] * 5,
        out_specs=anywhere,
        scratch_shapes=[
            pltpu.VMEM((chunks, rows, WIDTH), f32),
            pltpu.VMEM((levels + 1, chunks, width, WIDTH), f32),
            pltpu.VMEM((levels + 1, chunks, width, WIDTH), f32),
            pltpu.VMEM((levels, width, width), f32),
            pltpu.VMEM((levels, width, width), f32),
            pltpu.VMEM((rows, width), f32),
            pltpu.VMEM((width, width), f32),
            pltpu.VMEM((3, width, width), f32),
            pltpu.VMEM((levels, width, 3 * width), bf16),
            pltpu.VMEM((levels, width, 3 * width), bf16),
            pltpu.VMEM((2, width, 3 * width), bf16),
            pltpu.VMEM((2, width, 3 * width), bf16),
            pltpu.VMEM((rows, 3 * width), bf16),
            pltpu.VMEM((width, 3 * rows), bf16),
            dma((chunks,)),
            dma((chunks,)),
            dma((chunks,)),
            dma((levels,)),
            dma((levels,)),
            dma,
            dma,
            dma,
            dma,
            dma((3,)),
            dma((3,)),
            dma((levels + 1, chunks)),
            dma((levels + 1, chunks)),
        ],
        compiler_params=pltpu.CompilerParams(
            collective_id=0, has_side_effects=True, vmem_limit_bytes=62 * 1024 * 1024
        ),
    )(rhs, leaf_v, leaf_t, merge_v, merge_t)


def solution(mesh):
    return jax.shard_map(
        body,
        mesh=mesh,
        in_specs=(
            P("rows", "cols"),
            P(("rows", "cols"), None),
            P("rows", None),
            P(None, "rows", None),
            P(None, "rows", None),
        ),
        out_specs=P("rows", "cols"),
        check_vma=False,
    )
```
